32 devices in a mesh: batch: 8 (over y, x, core), seq: 4 (over z).
Axes of the slice: x: 2, y: 2, z: 4, core: 2. Of those that a mesh axis runs over, the one named last changes fastest.
Arguments:
- events: bfloat16 [8192, 256], P(('batch', 'seq')), parts along dimension 0, may hold values from -6 to 6
- positions: int32 [8192], P(('batch', 'seq')), parts along dimension 0, may hold values from 0 to 1023, as said below
- length: int32 [8], P('batch'), parts along dimension 0, may hold values from 512 to 1024
- filters: float32 [1024, 2, 256], P('seq'), may hold values from -0.1875 to 0.1875
- skip_gain: float32 [2, 256], replicated, may hold values from 0.5 to 1.5
- short_filter: float32 [3, 768], replicated, may hold values from -3 to 3
- in_proj: bfloat16 [256, 768], replicated, may hold values from -0.375 to 0.375
- out_proj: bfloat16 [256, 256], replicated, may hold values from -0.375 to 0.375
Outputs:
- layer_out: bfloat16 [8192, 256], P(('batch', 'seq')), parts along dimension 0
The draws below stay inside these ranges and needn't reach their ends.
There are 8 independent parts, one for each index of `batch`. The reference program is written for one: setup_inputs(seed, part) draws one part's arguments, and reference() takes and returns one part's arrays. A program takes and returns all parts, laid end to end along the dimension named above; an argument that names none is the same for every part. Nothing has to cross between parts.
Inputs may be any that keep to these rules, and one draw needn't show every extreme that they name: positions is a permutation of 0 to 1023. Cut each row block b (positions b * 256 to (b + 1) * 256 - 1) into runs of 64 positions, run c starting at b * 256 + c * 64. The rows of one seq device hold whole runs only, exactly one run of each row block and exactly one run of each index c, in any order.
All inputs are finite; a program needn't handle non-finite values.
Results may differ from the reference program's by a relative error of at most 0.007.
Values may be sent and summed in bfloat16 or wider, within the bound.
No kernel may reach another device: no remote copies, remote signals or barrier semaphores. Data moves between devices by JAX's collectives and lax.ppermute only.
A program may use at most 64 MiB of HBM per device.

```python
import jax
import jax.numpy as jnp

D = 256
TOK_DEV = 256
TOKENS = 1024
N_SEQ = 4


def draw_positions(key, part):
    key_rows, key_cols, key_order = jax.random.split(key, 3)
    col_size = TOK_DEV // N_SEQ
    row_shift = jax.random.permutation(key_rows, N_SEQ)
    col_shift = jax.random.permutation(key_cols, N_SEQ)
    col_inverse = jnp.argsort(col_shift)
    source_ids = jnp.arange(N_SEQ, dtype=jnp.int32)[:, None]
    block_ids = jnp.arange(N_SEQ, dtype=jnp.int32)[None, :]
    column_ids = col_inverse[(source_ids - row_shift[block_ids]) % N_SEQ]
    starts = block_ids * TOK_DEV + column_ids * col_size
    offsets = jnp.arange(col_size, dtype=jnp.int32)[None, None, :]
    placed = (starts[:, :, None] + offsets).reshape(N_SEQ, TOK_DEV)
    row_keys = jax.random.split(key_order, N_SEQ)
    shuffles = jax.vmap(lambda one_key: jax.random.permutation(one_key, TOK_DEV))(row_keys)
    placed = jnp.take_along_axis(placed, shuffles, axis=1)
    return placed.reshape(-1).astype(jnp.int32)


def block_levels(own_key, shape, cuts, least, largest):
    level = 1.0
    for position, blocks in cuts:
        heights = jax.random.uniform(jax.random.fold_in(jax.random.fold_in(own_key, 6), position), (blocks,), jnp.float32, least / len(cuts), largest / len(cuts))
        level = level * jnp.repeat(jnp.exp(heights), shape[position] // blocks).reshape((-1,) + (1,) * (len(shape) - 1 - position))
    return level


def centred(rng, shape, spread, most, cuts=(), held_as=jnp.bfloat16):
    entries = jax.random.normal(rng, shape, jnp.float32) * spread
    if len(cuts) > 0:
        entries = block_levels(rng, shape, cuts, -0.22, 0.18) * entries
    return jnp.clip(entries, min=-most, max=most).astype(held_as)


def setup_inputs(seed: int = 0, part: int = 0) -> dict:
    key_list = jax.random.split(jax.random.key(seed), 9)
    part_keys = jax.random.split(jax.random.fold_in(key_list[8], part), 9)
    return {
        "events": centred(part_keys[0], (TOKENS, D), 1.0, 6.0, ((0, 4),)),
        "positions": draw_positions(jax.random.fold_in(jax.random.fold_in(key_list[8], part), 71), part),
        "length": jax.random.randint(part_keys[2], (1,), TOKENS // 2, TOKENS + 1).astype(jnp.int32),
        "filters": centred(key_list[3], (TOKENS, 2, D), TOKENS ** -0.5, 0.1875, ((0, 4),), jnp.float32),
        "skip_gain": jnp.clip(jax.random.uniform(key_list[4], (2, D), jnp.float32, 0.5, 1.5), 0.5, 1.5),
        "short_filter": centred(key_list[5], (3, 3 * D), 0.6, 3.0, (), jnp.float32),
        "in_proj": centred(key_list[6], (D, 3 * D), D ** -0.5, 0.375),
        "out_proj": centred(key_list[7], (D, D), D ** -0.5, 0.375),
    }


def long_conv(signal, taps):
    padded_len = 2 * signal.shape[0]
    spectrum = jnp.fft.rfft(signal, n=padded_len, axis=0) * jnp.fft.rfft(taps, n=padded_len, axis=0)
    return jnp.fft.irfft(spectrum, n=padded_len, axis=0)[:signal.shape[0]].astype(jnp.float32)


def reference(events, positions, length, filters, skip_gain, short_filter, in_proj, out_proj):
    stream = jnp.zeros_like(events).at[positions].set(events)
    keep_rows = (jnp.arange(TOKENS, dtype=jnp.int32) < length[0])[:, None]
    stream = jnp.where(keep_rows, stream, jnp.zeros_like(stream))
    projected = jnp.dot(stream, in_proj, preferred_element_type=jnp.float32).astype(jnp.bfloat16)
    widened = projected.astype(jnp.float32)
    padded = jnp.pad(widened, ((2, 0), (0, 0)))
    shorted = short_filter[0] * widened + short_filter[1] * padded[1:-1] + short_filter[2] * padded[:-2]
    value = shorted[:, :D]
    gate_one = shorted[:, D:2 * D]
    gate_two = shorted[:, 2 * D:]
    first = gate_one * (long_conv(value, filters[:, 0]) + skip_gain[0] * value)
    second = long_conv(first, filters[:, 1]) + skip_gain[1] * first
    gated = (gate_two * second).astype(jnp.bfloat16)
    return jnp.dot(gated, out_proj, preferred_element_type=jnp.float32).astype(jnp.bfloat16)
```

```python
import functools
import math

import jax
import jax.numpy as jnp
import numpy as np
from jax import lax
from jax.experimental import pallas as pl
from jax.experimental.pallas import tpu as pltpu
from jax.sharding import PartitionSpec as P

F32 = jnp.float32
BF16 = jnp.bfloat16
META = 16
NT = (((1,), (1,)), ((), ()))
NN = (((1,), (0,)), ((), ()))
TN = (((0,), (0,)), ((), ()))


def tables(dev_count, tok_rows):
    total = dev_count * tok_rows
    index = np.arange(tok_rows)
    angle = 2.0 * np.pi * (np.outer(index, index) % tok_rows) / tok_rows
    cos, sin = np.cos(angle), np.sin(angle)
    matrix = np.block([[cos, -sin], [sin, cos]]).astype(np.float32)
    high = matrix.astype(BF16)
    low = (matrix - high.astype(np.float32)).astype(BF16)
    twist = 2.0 * np.pi * (np.outer(4 * np.arange(dev_count) + 1, index) % (4 * total)) / (4 * total)
    twists = np.concatenate([np.cos(twist), np.sin(twist)], axis=0).astype(np.float32)
    return high, low, twists


def outer_coefficients(dev_count):
    angle = 2.0 * np.pi * np.outer(4 * np.arange(dev_count) + 1, np.arange(dev_count)) / (4 * dev_count)
    return np.cos(angle), np.sin(angle)


def split(x):
    high = x.astype(BF16)
    return high, (x - high.astype(F32)).astype(BF16)


def product(left_high, left_low, high_ref, low_ref, dims):
    dot = functools.partial(lax.dot_general, dimension_numbers=dims, preferred_element_type=F32)
    high = high_ref[...]
    return dot(left_high, high) + (dot(left_low, high) + dot(left_high, low_ref[...]))


def forward(blocks, high_ref, low_ref, twist_ref):
    count = len(blocks)
    inner = blocks[0].shape[1]
    cos, sin = outer_coefficients(count)
    reals, imags = [], []
    for k in range(count):
        real = blocks[0]
        imag = None
        for n in range(1, count):
            real = real + float(cos[k, n]) * blocks[n]
            term = float(-sin[k, n]) * blocks[n]
            imag = term if imag is None else imag + term
        turn_cos = twist_ref[k : k + 1, :]
        turn_sin = twist_ref[count + k : count + k + 1, :]
        if imag is None:
            imag = jnp.zeros_like(real)
        reals.append(real * turn_cos + imag * turn_sin)
        imags.append(imag * turn_cos - real * turn_sin)
    stacked = jnp.concatenate(
        [jnp.concatenate(reals, axis=0), jnp.concatenate(imags, axis=0)], axis=1
    )
    high, low = split(stacked)
    out = product(high, low, high_ref, low_ref, NN)
    return out[:, :inner], out[:, inner:]


def inverse(real, imag, count, high_ref, low_ref, twist_ref):
    inner = real.shape[1]
    width = real.shape[0] // count
    cos, sin = outer_coefficients(count)
    high, low = split(jnp.concatenate([real, imag], axis=1))
    out = product(high, low, high_ref, low_ref, NT)
    back_real, back_imag = out[:, :inner], out[:, inner:]
    scale = 1.0 / (count * inner)
    turned = []
    for k in range(count):
        rows = slice(k * width, (k + 1) * width)
        turn_cos = twist_ref[k : k + 1, :] * scale
        turn_sin = twist_ref[count + k : count + k + 1, :] * scale
        turned.append(
            (
                back_real[rows] * turn_cos - back_imag[rows] * turn_sin,
                back_imag[rows] * turn_cos + back_real[rows] * turn_sin,
            )
        )
    blocks = []
    for n in range(count):
        total = None
        for k in range(count):
            term = turned[k][0] if n == 0 else float(cos[k, n]) * turned[k][0] - float(sin[k, n]) * turned[k][1]
            total = term if total is None else total + term
        blocks.append(total)
    return blocks


def filter_kernel(count, filt_ref, *refs):
    outs, flipped = refs[:count], refs[count]
    me = lax.axis_index("seq")
    core = lax.rem(lax.axis_index("batch"), 2)
    width = outs[0].shape[0]
    one = jnp.where(core == 0, filt_ref[:, 0, :], filt_ref[:, 1, :])
    flipped[...] = one.T
    for k in range(count):
        start = pl.multiple_of(lax.bitwise_xor(me, k) * width, width)
        outs[k][...] = flipped[pl.ds(start, width), :]


def project_kernel(count, length_ref, events_ref, pos_ref, weights_ref, *refs):
    outs, whole = refs[:count], refs[count]
    me = lax.axis_index("seq")
    rows, features = events_ref.shape
    width = features // count
    pos = pos_ref[...]
    keep = (pos < length_ref[0]).astype(F32)
    projected = lax.dot_general(
        weights_ref[...], events_ref[...], (((0,), (1,)), ((), ())), preferred_element_type=F32
    )
    whole[...] = (projected * keep).astype(BF16)
    line = lax.broadcasted_iota(jnp.int32, (META, rows), 0)
    high = lax.div(pos, 256)
    meta = jnp.where(line == 0, high, jnp.where(line == 1, pos - high * 256, 0))
    meta = meta.astype(F32).astype(BF16)
    for k in range(count):
        dest = lax.bitwise_xor(me, k)
        for part in range(3):
            start = pl.multiple_of(part * features + dest * width, width)
            outs[k][part * width : (part + 1) * width, :] = whole[pl.ds(start, width), :]
        outs[k][3 * width :, :] = meta


def spectrum_kernel(count, high_ref, low_ref, twist_ref, short_ref, gain_ref, *refs):
    parts, spec_ref, scale_ref, held = refs[:count], refs[count], refs[count + 1], refs[count + 2]
    me = lax.axis_index("seq")
    width, inner = parts[0].shape
    for k in range(count):
        held[pl.ds(lax.bitwise_xor(me, k), 1)] = parts[k][...][None]
    real, imag = forward([held[n] for n in range(count)], high_ref, low_ref, twist_ref)
    spec_ref[:, :inner] = real
    spec_ref[:, inner:] = imag
    features = gain_ref.shape[1]
    row = lax.broadcasted_iota(jnp.int32, (width, features), 0)
    lane = lax.broadcasted_iota(jnp.int32, (width, features), 1)
    chosen = lane == row + me * width
    place = lax.broadcasted_iota(jnp.int32, (width, scale_ref.shape[1]), 1)

    def column(line):
        return jnp.sum(jnp.where(chosen, line, 0.0), axis=1, keepdims=True)

    for part in range(3):
        out = jnp.zeros((width, scale_ref.shape[1]), F32)
        for tap in range(3):
            line = short_ref[tap : tap + 1, part * features : (part + 1) * features]
            out = jnp.where(place == tap, column(line), out)
        if part < 2:
            out = jnp.where(place == 3, column(gain_ref[part : part + 1, :]), out)
        scale_ref[part * width : (part + 1) * width, :] = out


def mix_kernel(count, high_ref, low_ref, twist_ref, scale_ref, own_ref, other_ref, *refs):
    parts, outs, gated = refs[:count], refs[count : 2 * count], refs[2 * count]
    me = lax.axis_index("seq")
    core = lax.rem(lax.axis_index("batch"), 2)
    inner = parts[0].shape[1]
    width = (parts[0].shape[0] - META) // 3
    rows = [part[: 3 * width, :] for part in parts]
    places = []
    for part in parts:
        meta = part[3 * width :, :].astype(F32)
        places.append((meta[0:1, :] * 256.0 + meta[1:2, :]).astype(jnp.int32))
    wanted = lax.broadcasted_iota(jnp.int32, (inner, inner), 0)
    placed = []
    for n in range(count):
        total = None
        for k in range(count):
            hit = (wanted + n * inner == places[k]).astype(F32).astype(BF16)
            term = lax.dot_general(rows[k], hit, NT, preferred_element_type=F32)
            total = term if total is None else total + term
        placed.append(total)
    whole = jnp.concatenate(placed, axis=1)
    lane = lax.broadcasted_iota(jnp.int32, (1, count * inner), 1)
    scale = scale_ref[...]
    back_one = jnp.where(lane >= 1, pltpu.roll(whole, 1, 1), 0.0)
    back_two = jnp.where(lane >= 2, pltpu.roll(whole, 2, 1), 0.0)
    shorted = scale[:, 0:1] * whole + scale[:, 1:2] * back_one + scale[:, 2:3] * back_two

    def blocks_of(part):
        return [
            shorted[part * width : (part + 1) * width, n * inner : (n + 1) * inner]
            for n in range(count)
        ]

    def spectrum(which):
        mine = core == which
        return jnp.where(mine, own_ref[...], other_ref[...])

    def convolve(blocks, which):
        taps = spectrum(which)
        taps_real, taps_imag = taps[:, :inner], taps[:, inner:]
        real, imag = forward(blocks, high_ref, low_ref, twist_ref)
        return inverse(
            real * taps_real - imag * taps_imag,
            real * taps_imag + imag * taps_real,
            count, high_ref, low_ref, twist_ref,
        )

    value, gate_one, gate_two = blocks_of(0), blocks_of(1), blocks_of(2)
    gain_one, gain_two = scale[:width, 3:4], scale[width : 2 * width, 3:4]
    mixed = convolve(value, 0)
    first = [gate_one[n] * (mixed[n] + gain_one * value[n]) for n in range(count)]
    mixed = convolve(first, 1)
    for n in range(count):
        gated[n] = (gate_two[n] * (mixed[n] + gain_two * first[n])).astype(BF16)
    for k in range(count):
        outs[k][...] = gated[pl.ds(lax.bitwise_xor(me, k), 1)][0]


def output_kernel(count, weights_ref, *refs):
    parts, out_ref = refs[:count], refs[count]
    me = lax.axis_index("seq")
    width = parts[0].shape[0]
    total = None
    for k in range(count):
        start = pl.multiple_of(lax.bitwise_xor(me, k) * width, width)
        term = lax.dot_general(
            parts[k][...], weights_ref[pl.ds(start, width), :], TN, preferred_element_type=F32
        )
        total = term if total is None else total + term
    out_ref[...] = total.astype(BF16)


def call(kernel, name, out_shape, scratch, flops, *args):
    smem = pl.BlockSpec(memory_space=pltpu.SMEM)
    vmem = pl.BlockSpec(memory_space=pltpu.VMEM)
    outs = out_shape if isinstance(out_shape, (list, tuple)) else [out_shape]
    moved = sum(math.prod(a.shape) * a.dtype.itemsize for a in list(args) + list(outs))
    return pl.pallas_call(
        kernel,
        name=name,
        out_shape=out_shape,
        in_specs=[smem if a.ndim == 1 else vmem for a in args],
        out_specs=jax.tree.map(lambda _: vmem, out_shape),
        scratch_shapes=scratch,
        cost_estimate=pl.CostEstimate(flops=flops, bytes_accessed=moved, transcendentals=0),
        compiler_params=pltpu.CompilerParams(vmem_limit_bytes=48 * 1024 * 1024),
    )(*args)


def exchange(parts):
    count = len(parts)
    got = [parts[0]]
    for k in range(1, count):
        got.append(lax.ppermute(parts[k], "seq", [(d, d ^ k) for d in range(count)]))
    return got


def body(events, positions, length, filters, skip_gain, short_filter, in_proj, out_proj):
    tok_rows, features = events.shape
    count = lax.axis_size("seq")
    width = features // count
    shape = jax.ShapeDtypeStruct
    high, low, twists = (jnp.asarray(t) for t in tables(count, tok_rows))

    filter_parts = call(
        functools.partial(filter_kernel, count), "filters",
        [shape((width, tok_rows), F32)] * count,
        [pltpu.VMEM((features, tok_rows), F32)], 10**6, filters,
    )
    filter_parts = exchange(filter_parts)
    sent = call(
        functools.partial(project_kernel, count), "project",
        [shape((3 * width + META, tok_rows), BF16)] * count,
        [pltpu.VMEM((3 * features, tok_rows), BF16)], 10**8,
        length, events, positions.reshape(1, tok_rows), in_proj,
    )
    got = exchange(sent)
    own, scale = call(
        functools.partial(spectrum_kernel, count), "spectrum",
        [shape((features, 2 * tok_rows), F32), shape((3 * width, 128), F32)],
        [pltpu.VMEM((count, width, tok_rows), F32)], 4 * 10**8,
        high, low, twists, short_filter, skip_gain, *filter_parts,
    )
    pairs = [(d, d ^ 1) for d in range(lax.axis_size("batch"))]
    other = lax.ppermute(own, "batch", pairs)
    gated = call(
        functools.partial(mix_kernel, count), "mix",
        [shape((width, tok_rows), BF16)] * count,
        [pltpu.VMEM((count, width, tok_rows), BF16)], 2 * 10**9,
        high, low, twists, scale, own, other, *got,
    )
    back = exchange(gated)
    return call(
        functools.partial(output_kernel, count), "output",
        shape((tok_rows, features), BF16), [], 10**8, out_proj, *back,
    )


def solution(mesh):
    return jax.shard_map(
        body,
        mesh=mesh,
        in_specs=(
            P(("batch", "seq"), None),
            P(("batch", "seq")),
            P("batch"),
            P("seq", None, None),
            P(),
            P(),
            P(),
            P(),
        ),
        out_specs=P(("batch", "seq"), None),
        check_vma=False,
    )
```

```python
import functools
import math

import jax
import jax.numpy as jnp
import numpy as np
from jax import lax
from jax.experimental import pallas as pl
from jax.experimental.pallas import tpu as pltpu
from jax.sharding import PartitionSpec as P

F32 = jnp.float32
BF16 = jnp.bfloat16
META = 16
NT = (((1,), (1,)), ((), ()))
NN = (((1,), (0,)), ((), ()))
TN = (((0,), (0,)), ((), ()))


def tables(dev_count, tok_rows):
    total = dev_count * tok_rows
    index = np.arange(tok_rows)
    angle = 2.0 * np.pi * (np.outer(index, index) % tok_rows) / tok_rows
    cos, sin = np.cos(angle), np.sin(angle)
    matrix = np.block([[cos, -sin], [sin, cos]]).astype(np.float32)
    high = matrix.astype(BF16)
    low = (matrix - high.astype(np.float32)).astype(BF16)
    twist = 2.0 * np.pi * (np.outer(4 * np.arange(dev_count) + 1, index) % (4 * total)) / (4 * total)
    twists = np.concatenate([np.cos(twist), np.sin(twist)], axis=0).astype(np.float32)
    return high, low, twists


def outer_coefficients(dev_count):
    angle = 2.0 * np.pi * np.outer(4 * np.arange(dev_count) + 1, np.arange(dev_count)) / (4 * dev_count)
    return np.cos(angle), np.sin(angle)


def split(x):
    high = x.astype(BF16)
    return high, (x - high.astype(F32)).astype(BF16)


def product(left_high, left_low, high_ref, low_ref, dims):
    dot = functools.partial(lax.dot_general, dimension_numbers=dims, preferred_element_type=F32)
    high = high_ref[...]
    return dot(left_high, high) + (dot(left_low, high) + dot(left_high, low_ref[...]))


def forward(blocks, high_ref, low_ref, twist_ref):
    count = len(blocks)
    inner = blocks[0].shape[1]
    cos, sin = outer_coefficients(count)
    reals, imags = [], []
    for k in range(count):
        real = blocks[0]
        imag = None
        for n in range(1, count):
            real = real + float(cos[k, n]) * blocks[n]
            term = float(-sin[k, n]) * blocks[n]
            imag = term if imag is None else imag + term
        turn_cos = twist_ref[k : k + 1, :]
        turn_sin = twist_ref[count + k : count + k + 1, :]
        if imag is None:
            imag = jnp.zeros_like(real)
        reals.append(real * turn_cos + imag * turn_sin)
        imags.append(imag * turn_cos - real * turn_sin)
    stacked = jnp.concatenate(
        [jnp.concatenate(reals, axis=0), jnp.concatenate(imags, axis=0)], axis=1
    )
    high, low = split(stacked)
    out = product(high, low, high_ref, low_ref, NN)
    return out[:, :inner], out[:, inner:]


def inverse(real, imag, count, high_ref, low_ref, twist_ref):
    inner = real.shape[1]
    width = real.shape[0] // count
    cos, sin = outer_coefficients(count)
    high, low = split(jnp.concatenate([real, imag], axis=1))
    out = product(high, low, high_ref, low_ref, NT)
    back_real, back_imag = out[:, :inner], out[:, inner:]
    scale = 1.0 / (count * inner)
    turned = []
    for k in range(count):
        rows = slice(k * width, (k + 1) * width)
        turn_cos = twist_ref[k : k + 1, :] * scale
        turn_sin = twist_ref[count + k : count + k + 1, :] * scale
        turned.append(
            (
                back_real[rows] * turn_cos - back_imag[rows] * turn_sin,
                back_imag[rows] * turn_cos + back_real[rows] * turn_sin,
            )
        )
    blocks = []
    for n in range(count):
        total = None
        for k in range(count):
            term = turned[k][0] if n == 0 else float(cos[k, n]) * turned[k][0] - float(sin[k, n]) * turned[k][1]
            total = term if total is None else total + term
        blocks.append(total)
    return blocks


def prepare_kernel(count, events_hbm, pos_hbm, weights_hbm, filt_hbm, *refs):
    taps, rows_out = refs[:count], refs[count : 2 * count]
    events_ref, pos_ref, weights_ref, filt_ref, flipped, whole, sems = refs[2 * count :]
    me = lax.axis_index("seq")
    core = lax.rem(lax.axis_index("batch"), 2)
    loads = [
        pltpu.make_async_copy(source, target, sems.at[n])
        for n, (source, target) in enumerate((
            (events_hbm, events_ref),
            (weights_hbm, weights_ref),
            (filt_hbm, filt_ref),
            (pos_hbm, pos_ref),
        ))
    ]
    for load in loads:
        load.start()
    rows, features = events_ref.shape
    width = features // count
    loads[2].wait()
    one = jnp.where(core == 0, filt_ref[:, 0, :], filt_ref[:, 1, :])
    flipped[...] = one.T
    for k in range(count):
        start = pl.multiple_of(lax.bitwise_xor(me, k) * width, width)
        taps[k][...] = flipped[pl.ds(start, width), :]
    for n in (0, 1, 3):
        loads[n].wait()
    pos = pos_ref[...]
    projected = lax.dot_general(
        weights_ref[...], events_ref[...], (((0,), (1,)), ((), ())), preferred_element_type=F32
    )
    whole[...] = projected.astype(BF16)
    line = lax.broadcasted_iota(jnp.int32, (META, rows), 0)
    high = lax.div(pos, 256)
    meta = jnp.where(line == 0, high, jnp.where(line == 1, pos - high * 256, 0))
    meta = meta.astype(F32).astype(BF16)
    for k in range(count):
        dest = lax.bitwise_xor(me, k)
        for part in range(3):
            start = pl.multiple_of(part * features + dest * width, width)
            rows_out[k][part * width : (part + 1) * width, :] = whole[pl.ds(start, width), :]
        rows_out[k][3 * width :, :] = meta


def spectrum_kernel(count, high_ref, low_ref, twist_ref, short_ref, gain_ref, length_ref, *refs):
    parts, spec_ref, scale_ref, held = refs[:count], refs[count], refs[count + 1], refs[count + 2]
    me = lax.axis_index("seq")
    width, inner = parts[0].shape
    for k in range(count):
        held[pl.ds(lax.bitwise_xor(me, k), 1)] = parts[k][...][None]
    real, imag = forward([held[n] for n in range(count)], high_ref, low_ref, twist_ref)
    spec_ref[:, :inner] = real
    spec_ref[:, inner:] = imag
    features = gain_ref.shape[1]
    row = lax.broadcasted_iota(jnp.int32, (width, features), 0)
    lane = lax.broadcasted_iota(jnp.int32, (width, features), 1)
    chosen = lane == row + me * width
    place = lax.broadcasted_iota(jnp.int32, (width, scale_ref.shape[1]), 1)

    def column(line):
        return jnp.sum(jnp.where(chosen, line, 0.0), axis=1, keepdims=True)

    for part in range(3):
        out = jnp.zeros((width, scale_ref.shape[1]), F32)
        for tap in range(3):
            line = short_ref[tap : tap + 1, part * features : (part + 1) * features]
            out = jnp.where(place == tap, column(line), out)
        if part < 2:
            out = jnp.where(place == 3, column(gain_ref[part : part + 1, :]), out)
        out = jnp.where(place == 4, length_ref[...].astype(F32), out)
        scale_ref[part * width : (part + 1) * width, :] = out


def mix_kernel(count, high_ref, low_ref, twist_ref, scale_ref, own_ref, other_ref, *refs):
    parts, outs, gated = refs[:count], refs[count : 2 * count], refs[2 * count]
    me = lax.axis_index("seq")
    core = lax.rem(lax.axis_index("batch"), 2)
    inner = parts[0].shape[1]
    width = (parts[0].shape[0] - META) // 3
    rows = [part[: 3 * width, :] for part in parts]
    places = []
    for part in parts:
        meta = part[3 * width :, :].astype(F32)
        places.append((meta[0:1, :] * 256.0 + meta[1:2, :]).astype(jnp.int32))
    wanted = lax.broadcasted_iota(jnp.int32, (inner, inner), 0)
    placed = []
    for n in range(count):
        total = None
        for k in range(count):
            hit = (wanted + n * inner == places[k]).astype(F32).astype(BF16)
            term = lax.dot_general(rows[k], hit, NT, preferred_element_type=F32)
            total = term if total is None else total + term
        placed.append(total)
    lane = lax.broadcasted_iota(jnp.int32, (1, count * inner), 1)
    scale = scale_ref[...]
    real_rows = lane.astype(F32) < scale[0:1, 4:5]
    whole = jnp.where(real_rows, jnp.concatenate(placed, axis=1), 0.0)
    back_one = jnp.where(lane >= 1, pltpu.roll(whole, 1, 1), 0.0)
    back_two = jnp.where(lane >= 2, pltpu.roll(whole, 2, 1), 0.0)
    shorted = scale[:, 0:1] * whole + scale[:, 1:2] * back_one + scale[:, 2:3] * back_two

    def blocks_of(part):
        return [
            shorted[part * width : (part + 1) * width, n * inner : (n + 1) * inner]
            for n in range(count)
        ]

    def spectrum(which):
        mine = core == which
        return jnp.where(mine, own_ref[...], other_ref[...])

    def convolve(blocks, which):
        taps = spectrum(which)
        taps_real, taps_imag = taps[:, :inner], taps[:, inner:]
        real, imag = forward(blocks, high_ref, low_ref, twist_ref)
        return inverse(
            real * taps_real - imag * taps_imag,
            real * taps_imag + imag * taps_real,
            count, high_ref, low_ref, twist_ref,
        )

    value, gate_one, gate_two = blocks_of(0), blocks_of(1), blocks_of(2)
    gain_one, gain_two = scale[:width, 3:4], scale[width : 2 * width, 3:4]
    mixed = convolve(value, 0)
    first = [gate_one[n] * (mixed[n] + gain_one * value[n]) for n in range(count)]
    mixed = convolve(first, 1)
    for n in range(count):
        gated[n] = (gate_two[n] * (mixed[n] + gain_two * first[n])).astype(BF16)
    for k in range(count):
        outs[k][...] = gated[pl.ds(lax.bitwise_xor(me, k), 1)][0]


def output_kernel(count, weights_ref, *refs):
    parts, out_ref = refs[:count], refs[count]
    me = lax.axis_index("seq")
    width = parts[0].shape[0]
    total = None
    for k in range(count):
        start = pl.multiple_of(lax.bitwise_xor(me, k) * width, width)
        term = lax.dot_general(
            parts[k][...], weights_ref[pl.ds(start, width), :], TN, preferred_element_type=F32
        )
        total = term if total is None else total + term
    out_ref[...] = total.astype(BF16)


def call(kernel, out_shape, scratch, flops, space, *args, grant=48 * 1024 * 1024):
    vmem = pl.BlockSpec(memory_space=pltpu.VMEM)
    outs = out_shape if isinstance(out_shape, (list, tuple)) else [out_shape]
    moved = sum(math.prod(a.shape) * a.dtype.itemsize for a in list(args) + list(outs))
    return pl.pallas_call(
        kernel,
        out_shape=out_shape,
        in_specs=[pl.BlockSpec(memory_space=space)] * len(args),
        out_specs=jax.tree.map(lambda _: vmem, out_shape),
        scratch_shapes=scratch,
        cost_estimate=pl.CostEstimate(flops=flops, bytes_accessed=moved, transcendentals=0),
        compiler_params=pltpu.CompilerParams(vmem_limit_bytes=grant),
    )(*args)


def exchange(parts):
    count = len(parts)
    got = [parts[0]]
    for k in range(1, count):
        got.append(lax.ppermute(parts[k], "seq", [(d, d ^ k) for d in range(count)]))
    return got


def body(events, positions, length, filters, skip_gain, short_filter, in_proj, out_proj):
    tok_rows, features = events.shape
    count = lax.axis_size("seq")
    width = features // count
    shape = jax.ShapeDtypeStruct
    high, low, twists = (jnp.asarray(t) for t in tables(count, tok_rows))

    prepared = call(
        functools.partial(prepare_kernel, count),
        [shape((width, tok_rows), F32)] * count
        + [shape((3 * width + META, tok_rows), BF16)] * count,
        [
            pltpu.VMEM(events.shape, BF16),
            pltpu.VMEM((1, tok_rows), jnp.int32),
            pltpu.VMEM(in_proj.shape, BF16),
            pltpu.VMEM(filters.shape, F32),
            pltpu.VMEM((features, tok_rows), F32),
            pltpu.VMEM((3 * features, tok_rows), BF16),
            pltpu.SemaphoreType.DMA((4,)),
        ],
        10**8, pltpu.HBM, events, positions.reshape(1, tok_rows), in_proj, filters,
        grant=65500000,
    )
    filter_parts = exchange(prepared[:count])
    got = exchange(prepared[count:])
    own, scale = call(
        functools.partial(spectrum_kernel, count),
        [shape((features, 2 * tok_rows), F32), shape((3 * width, 128), F32)],
        [pltpu.VMEM((count, width, tok_rows), F32)], 4 * 10**8, pltpu.VMEM,
        high, low, twists, short_filter, skip_gain, length.reshape(1, 1), *filter_parts,
    )
    pairs = [(d, d ^ 1) for d in range(lax.axis_size("batch"))]
    other = lax.ppermute(own, "batch", pairs)
    gated = call(
        functools.partial(mix_kernel, count),
        [shape((width, tok_rows), BF16)] * count,
        [pltpu.VMEM((count, width, tok_rows), BF16)], 2 * 10**9, pltpu.VMEM,
        high, low, twists, scale, own, other, *got,
    )
    back = exchange(gated)
    return call(
        functools.partial(output_kernel, count),
        shape((tok_rows, features), BF16), [], 10**8, pltpu.VMEM, out_proj, *back,
    )


def solution(mesh):
    return jax.shard_map(
        body,
        mesh=mesh,
        in_specs=(
            P(("batch", "seq"), None),
            P(("batch", "seq")),
            P("batch"),
            P("seq", None, None),
            P(),
            P(),
            P(),
            P(),
        ),
        out_specs=P(("batch", "seq"), None),
        check_vma=False,
    )
```

```python
import functools
import math

import jax
import jax.numpy as jnp
import numpy as np
from jax import lax
from jax.experimental import pallas as pl
from jax.experimental.pallas import tpu as pltpu
from jax.sharding import PartitionSpec as P

F32 = jnp.float32
BF16 = jnp.bfloat16
META = 8
NT = (((1,), (1,)), ((), ()))
NN = (((1,), (0,)), ((), ()))
TN = (((0,), (0,)), ((), ()))


def tables(dev_count, tok_rows):
    total = dev_count * tok_rows
    index = np.arange(tok_rows)
    angle = 2.0 * np.pi * (np.outer(index, index) % tok_rows) / tok_rows
    cos, sin = np.cos(angle), np.sin(angle)
    matrix = np.block([[cos, -sin], [sin, cos]]).astype(np.float32)
    high = matrix.astype(BF16)
    low = (matrix - high.astype(np.float32)).astype(BF16)
    twist = 2.0 * np.pi * (np.outer(4 * np.arange(dev_count) + 1, index) % (4 * total)) / (4 * total)
    twists = np.concatenate([np.cos(twist), np.sin(twist)], axis=0).astype(np.float32)
    return high, low, twists


def outer_coefficients(dev_count):
    angle = 2.0 * np.pi * np.outer(4 * np.arange(dev_count) + 1, np.arange(dev_count)) / (4 * dev_count)
    return np.cos(angle), np.sin(angle)


def split(x):
    high = x.astype(BF16)
    return high, (x - high.astype(F32)).astype(BF16)


def product(left_high, left_low, high_ref, low_ref, dims):
    dot = functools.partial(lax.dot_general, dimension_numbers=dims, preferred_element_type=F32)
    high = high_ref[...]
    return dot(left_high, high) + (dot(left_low, high) + dot(left_high, low_ref[...]))


def forward(blocks, high_ref, low_ref, twist_ref):
    count = len(blocks)
    inner = blocks[0].shape[1]
    cos, sin = outer_coefficients(count)
    reals, imags = [], []
    for k in range(count):
        real = blocks[0]
        imag = None
        for n in range(1, count):
            real = real + float(cos[k, n]) * blocks[n]
            term = float(-sin[k, n]) * blocks[n]
            imag = term if imag is None else imag + term
        turn_cos = twist_ref[k : k + 1, :]
        turn_sin = twist_ref[count + k : count + k + 1, :]
        if imag is None:
            imag = jnp.zeros_like(real)
        reals.append(real * turn_cos + imag * turn_sin)
        imags.append(imag * turn_cos - real * turn_sin)
    stacked = jnp.concatenate(
        [jnp.concatenate(reals, axis=0), jnp.concatenate(imags, axis=0)], axis=1
    )
    high, low = split(stacked)
    out = product(high, low, high_ref, low_ref, NN)
    return out[:, :inner], out[:, inner:]


def inverse(real, imag, count, high_ref, low_ref, twist_ref):
    inner = real.shape[1]
    width = real.shape[0] // count
    cos, sin = outer_coefficients(count)
    high, low = split(jnp.concatenate([real, imag], axis=1))
    out = product(high, low, high_ref, low_ref, NT)
    back_real, back_imag = out[:, :inner], out[:, inner:]
    scale = 1.0 / (count * inner)
    turned = []
    for k in range(count):
        rows = slice(k * width, (k + 1) * width)
        turn_cos = twist_ref[k : k + 1, :] * scale
        turn_sin = twist_ref[count + k : count + k + 1, :] * scale
        turned.append(
            (
                back_real[rows] * turn_cos - back_imag[rows] * turn_sin,
                back_imag[rows] * turn_cos + back_real[rows] * turn_sin,
            )
        )
    blocks = []
    for n in range(count):
        total = None
        for k in range(count):
            term = turned[k][0] if n == 0 else float(cos[k, n]) * turned[k][0] - float(sin[k, n]) * turned[k][1]
            total = term if total is None else total + term
        blocks.append(total)
    return blocks


def filter_kernel(count, filt_ref, *refs):
    taps, flipped = refs[:count], refs[count]
    me = lax.axis_index("seq")
    core = lax.rem(lax.axis_index("batch"), 2)
    half = lax.rem(lax.div(lax.axis_index("batch"), 2), 2)
    share = taps[0].shape[0]
    one = jnp.where(core == 0, filt_ref[:, 0, :], filt_ref[:, 1, :])
    flipped[...] = one.T
    for k in range(count):
        start = pl.multiple_of((2 * lax.bitwise_xor(me, k) + half) * share, share)
        taps[k][...] = flipped[pl.ds(start, share), :]


def project_kernel(count, events_ref, weights_ref, pos_ref, *refs):
    rows_out, whole = refs[:count], refs[count]
    me = lax.axis_index("seq")
    rows, features = events_ref.shape
    width = features // count
    projected = lax.dot_general(
        weights_ref[...], events_ref[...], (((0,), (1,)), ((), ())), preferred_element_type=F32
    )
    whole[...] = projected.astype(BF16)
    pos = pos_ref[...]
    line = lax.broadcasted_iota(jnp.int32, (META, rows), 0)
    high = lax.div(pos, 256)
    meta = jnp.where(line == 0, high, jnp.where(line == 1, pos - high * 256, 0))
    meta = meta.astype(F32).astype(BF16)
    for k in range(count):
        dest = lax.bitwise_xor(me, k)
        for part in range(3):
            start = pl.multiple_of(part * features + dest * width, width)
            rows_out[k][part * width : (part + 1) * width, :] = whole[pl.ds(start, width), :]
        rows_out[k][3 * width :, :] = meta


def gather_kernel(count, *refs):
    parts, out_ref = refs[:count], refs[count]
    me = lax.axis_index("seq")
    share = parts[0].shape[0]
    for k in range(count):
        start = pl.multiple_of(lax.bitwise_xor(me, k) * share, share)
        out_ref[pl.ds(start, share), :] = parts[k][...]


def spectrum_kernel(count, high_ref, low_ref, twist_ref, short_ref, gain_ref, length_ref, *refs):
    own_ref, other_ref, spec_ref, scale_ref = refs
    me = lax.axis_index("seq")
    half = lax.rem(lax.div(lax.axis_index("batch"), 2), 2)
    share, inner = own_ref.shape[0] // count, own_ref.shape[1]
    width = 2 * share
    own, other = own_ref[...], other_ref[...]
    lower, upper = jnp.where(half == 0, own, other), jnp.where(half == 0, other, own)
    blocks = [
        jnp.concatenate([part[n * share : (n + 1) * share] for part in (lower, upper)], axis=0)
        for n in range(count)
    ]
    real, imag = forward(blocks, high_ref, low_ref, twist_ref)
    spec_ref[:, :inner] = real
    spec_ref[:, inner:] = imag
    features = gain_ref.shape[1]
    row = lax.broadcasted_iota(jnp.int32, (width, features), 0)
    lane = lax.broadcasted_iota(jnp.int32, (width, features), 1)
    chosen = lane == row + me * width
    place = lax.broadcasted_iota(jnp.int32, (width, scale_ref.shape[1]), 1)

    def column(line):
        return jnp.sum(jnp.where(chosen, line, 0.0), axis=1, keepdims=True)

    for part in range(3):
        out = jnp.zeros((width, scale_ref.shape[1]), F32)
        for tap in range(3):
            line = short_ref[tap : tap + 1, part * features : (part + 1) * features]
            out = jnp.where(place == tap, column(line), out)
        if part < 2:
            out = jnp.where(place == 3, column(gain_ref[part : part + 1, :]), out)
        out = jnp.where(place == 4, length_ref[...].astype(F32), out)
        scale_ref[part * width : (part + 1) * width, :] = out


def mix_kernel(count, high_ref, low_ref, twist_ref, scale_ref, own_ref, other_ref, *refs):
    parts, outs, gated = refs[:count], refs[count : 2 * count], refs[2 * count]
    me = lax.axis_index("seq")
    core = lax.rem(lax.axis_index("batch"), 2)
    inner = parts[0].shape[1]
    width = (parts[0].shape[0] - META) // 3
    rows = [part[: 3 * width, :] for part in parts]
    places = []
    for part in parts:
        meta = part[3 * width :, :].astype(F32)
        places.append((meta[0:1, :] * 256.0 + meta[1:2, :]).astype(jnp.int32))
    wanted = lax.broadcasted_iota(jnp.int32, (inner, inner), 0)
    placed = []
    for n in range(count):
        total = None
        for k in range(count):
            hit = (wanted + n * inner == places[k]).astype(F32).astype(BF16)
            term = lax.dot_general(rows[k], hit, NT, preferred_element_type=F32)
            total = term if total is None else total + term
        placed.append(total)
    lane = lax.broadcasted_iota(jnp.int32, (1, count * inner), 1)
    scale = scale_ref[...]
    real_rows = lane.astype(F32) < scale[0:1, 4:5]
    whole = jnp.where(real_rows, jnp.concatenate(placed, axis=1), 0.0)
    back_one = jnp.where(lane >= 1, pltpu.roll(whole, 1, 1), 0.0)
    back_two = jnp.where(lane >= 2, pltpu.roll(whole, 2, 1), 0.0)
    shorted = scale[:, 0:1] * whole + scale[:, 1:2] * back_one + scale[:, 2:3] * back_two

    def blocks_of(part):
        return [
            shorted[part * width : (part + 1) * width, n * inner : (n + 1) * inner]
            for n in range(count)
        ]

    def spectrum(which):
        mine = core == which
        return jnp.where(mine, own_ref[...], other_ref[...])

    def convolve(blocks, which):
        taps = spectrum(which)
        taps_real, taps_imag = taps[:, :inner], taps[:, inner:]
        real, imag = forward(blocks, high_ref, low_ref, twist_ref)
        return inverse(
            real * taps_real - imag * taps_imag,
            real * taps_imag + imag * taps_real,
            count, high_ref, low_ref, twist_ref,
        )

    value, gate_one, gate_two = blocks_of(0), blocks_of(1), blocks_of(2)
    gain_one, gain_two = scale[:width, 3:4], scale[width : 2 * width, 3:4]
    mixed = convolve(value, 0)
    first = [gate_one[n] * (mixed[n] + gain_one * value[n]) for n in range(count)]
    mixed = convolve(first, 1)
    for n in range(count):
        gated[n] = (gate_two[n] * (mixed[n] + gain_two * first[n])).astype(BF16)
    for k in range(count):
        outs[k][...] = gated[pl.ds(lax.bitwise_xor(me, k), 1)][0]


def output_kernel(count, weights_ref, *refs):
    parts, out_ref = refs[:count], refs[count]
    me = lax.axis_index("seq")
    width = parts[0].shape[0]
    total = None
    for k in range(count):
        start = pl.multiple_of(lax.bitwise_xor(me, k) * width, width)
        term = lax.dot_general(
            parts[k][...], weights_ref[pl.ds(start, width), :], TN, preferred_element_type=F32
        )
        total = term if total is None else total + term
    out_ref[...] = total.astype(BF16)


def call(kernel, out_shape, scratch, flops, space, *args, grant=48 * 1024 * 1024):
    vmem = pl.BlockSpec(memory_space=pltpu.VMEM)
    outs = out_shape if isinstance(out_shape, (list, tuple)) else [out_shape]
    moved = sum(math.prod(a.shape) * a.dtype.itemsize for a in list(args) + list(outs))
    return pl.pallas_call(
        kernel,
        out_shape=out_shape,
        in_specs=[pl.BlockSpec(memory_space=space)] * len(args),
        out_specs=jax.tree.map(lambda _: vmem, out_shape),
        scratch_shapes=scratch,
        cost_estimate=pl.CostEstimate(flops=flops, bytes_accessed=moved, transcendentals=0),
        compiler_params=pltpu.CompilerParams(vmem_limit_bytes=grant),
    )(*args)


def hops(count):
    return [*range(count // 2, count), *range(1, count // 2)]


def exchange(parts):
    count = len(parts)
    got = [parts[0]] * count
    for k in hops(count):
        got[k] = lax.ppermute(parts[k], "seq", [(d, d ^ k) for d in range(count)])
    return got


def body(events, positions, length, filters, skip_gain, short_filter, in_proj, out_proj):
    tok_rows, features = events.shape
    count = lax.axis_size("seq")
    width = features // count
    shape = jax.ShapeDtypeStruct
    high, low, twists = (jnp.asarray(t) for t in tables(count, tok_rows))

    taps = call(
        functools.partial(filter_kernel, count),
        [shape((width // 2, tok_rows), F32)] * count,
        [pltpu.VMEM((features, tok_rows), F32)], 10**6, pltpu.VMEM, filters,
    )
    rows = call(
        functools.partial(project_kernel, count),
        [shape((3 * width + META, tok_rows), BF16)] * count,
        [pltpu.VMEM((3 * features, tok_rows), BF16)], 10**8, pltpu.VMEM,
        events, in_proj, positions.reshape(1, tok_rows),
    )
    filter_parts = exchange(taps)
    got = exchange(rows)
    groups = lax.axis_size("batch")
    half = call(
        functools.partial(gather_kernel, count),
        shape((features // 2, tok_rows), F32), [], 10**6, pltpu.VMEM, *filter_parts,
    )
    other_half = lax.ppermute(half, "batch", [(d, d ^ 2) for d in range(groups)])
    own, scale = call(
        functools.partial(spectrum_kernel, count),
        [shape((features, 2 * tok_rows), F32), shape((3 * width, 128), F32)],
        [], 4 * 10**8, pltpu.VMEM,
        high, low, twists, short_filter, skip_gain, length.reshape(1, 1), half, other_half,
    )
    pairs = [(d, d ^ 1) for d in range(groups)]
    other = lax.ppermute(own, "batch", pairs)
    gated = call(
        functools.partial(mix_kernel, count),
        [shape((width, tok_rows), BF16)] * count,
        [pltpu.VMEM((count, width, tok_rows), BF16)], 2 * 10**9, pltpu.VMEM,
        high, low, twists, scale, own, other, *got,
    )
    back = exchange(gated)
    return call(
        functools.partial(output_kernel, count),
        shape((tok_rows, features), BF16), [], 10**8, pltpu.VMEM, out_proj, *back,
    )


def solution(mesh):
    return jax.shard_map(
        body,
        mesh=mesh,
        in_specs=(
            P(("batch", "seq"), None),
            P(("batch", "seq")),
            P("batch"),
            P("seq", None, None),
            P(),
            P(),
            P(),
            P(),
        ),
        out_specs=P(("batch", "seq"), None),
        check_vma=False,
    )
```
